32 devices in a mesh: row: 8 (over z, y), col: 4 (over x, core).
Axes of the slice: x: 2, y: 2, z: 4, core: 2. Of those that a mesh axis runs over, the one named last changes fastest.
Arguments:
- grad_window: float32 [4096, 7168], P('row', 'col'), may hold values from -6 to 6
- rows_first: float32 [4096, 256], P('row'), may hold values from -0.09375 to 0.09375
- cols_first: float32 [7168, 256], P('col'), may hold values from -0.0625 to 0.0625
- rows_second: float32 [4096, 256], P('row'), may hold values from -0.09375 to 0.09375
- cols_second: float32 [7168, 256], P('col'), may hold values from -0.0625 to 0.0625
- inverse_first: float32 [256, 256], replicated, may hold values from -2 to 2, as said below
- inverse_second: float32 [256, 256], replicated, may hold values from -2 to 2, as said below
Outputs:
- panel_second: float32 [4096, 256], P('row')
- pivot_second: float32 [7168, 256], P('col')
- panel_first: float32 [4096, 256], P('row')
- pivot_first: float32 [7168, 256], P('col')
The draws below stay inside these ranges and needn't reach their ends.
Inputs may be any that keep to these rules, and one draw needn't show every extreme that they name: `inverse_first`: lower triangular, diagonal entries between 1 and 2. `inverse_second`: lower triangular, diagonal entries between 1 and 2.
All inputs are finite; a program needn't handle non-finite values.
Results may differ from the reference program's by a relative error of at most 0.000071.
Values sent between devices are 32-bit elements; how exact they have to be, the bound alone decides.
A program may use at most 64 MiB of HBM per device.

```python
import jax
import jax.numpy as jnp
from jax import lax

NB = 256
R = 4096
C = 7168


def lower_inverse(key):
    first_key, second_key = jax.random.split(key)
    diagonal = jax.random.uniform(first_key, (NB,), jnp.float32, 1.0, 2.0)
    spread = jnp.clip(jax.random.normal(second_key, (NB, NB), jnp.float32), -4.0, 4.0) * (0.5 * NB ** (-0.5))
    return jnp.tril(spread, -1) + jnp.diag(diagonal)


def draw_inverse_first(key, part):
    return lower_inverse(jax.random.fold_in(key, 11))


def draw_inverse_second(key, part):
    return lower_inverse(jax.random.fold_in(key, 23))


def block_levels(rng, shape, shards, least, top_value):
    def one(position, blocks):
        steps = jax.random.uniform(jax.random.fold_in(jax.random.fold_in(rng, 6), position), (blocks,), jnp.float32, least / len(shards), top_value / len(shards))
        return jnp.repeat(jnp.exp(steps), shape[position] // blocks).reshape((-1,) + (1,) * (len(shape) - position - 1))

    gain = one(*shards[0])
    for cut in shards[1:]:
        gain = gain * one(*cut)
    return gain


def bell_draw(key, dims, scale, limit, pieces=(), dtype=jnp.bfloat16):
    entries = scale * jax.random.normal(key, dims, jnp.float32)
    if pieces:
        entries = entries * block_levels(key, dims, pieces, -0.22, 0.18)
    return jnp.clip(entries, -limit, limit).astype(dtype)


def setup_inputs(seed: int = 0) -> dict:
    keys = jax.random.split(jax.random.key(seed), 8)
    grad_window = bell_draw(keys[0], (R, C), 1.0, 6.0, ((0, 8), (1, 4)), jnp.float32)
    rows_first = bell_draw(keys[1], (R, NB), R ** -0.5, 0.09375, ((0, 8),), jnp.float32)
    cols_first = bell_draw(keys[2], (C, NB), C ** -0.5, 0.0625, ((0, 4),), jnp.float32)
    rows_second = bell_draw(keys[3], (R, NB), R ** -0.5, 0.09375, ((0, 8),), jnp.float32)
    cols_second = bell_draw(keys[4], (C, NB), C ** -0.5, 0.0625, ((0, 4),), jnp.float32)
    inverse_first = draw_inverse_first(jax.random.fold_in(keys[7], 71), 0)
    inverse_second = draw_inverse_second(jax.random.fold_in(keys[7], 71), 0)
    return dict(grad_window=grad_window, rows_first=rows_first, cols_first=cols_first, rows_second=rows_second, cols_second=cols_second, inverse_first=inverse_first, inverse_second=inverse_second)


def matmul(left, right):
    return jnp.dot(left, right, precision=lax.Precision.HIGHEST, preferred_element_type=jnp.float32)


def reference(grad_window, rows_first, cols_first, rows_second, cols_second, inverse_first, inverse_second):
    left_second = -matmul(grad_window, cols_second)
    panel_second = matmul(left_second, inverse_second)
    pivot_second = matmul(-matmul(grad_window.T, rows_second), inverse_second)
    grad_next = grad_window.at[:, C - NB:].add(panel_second)
    panel_first = matmul(-matmul(grad_next, cols_first), inverse_first)
    pivot_first = matmul(-matmul(grad_next.T, rows_first), inverse_first)
    return panel_second, pivot_second, panel_first, pivot_first
```

```python
import functools

import jax
import jax.numpy as jnp
from jax import lax
from jax.experimental import pallas as pl
from jax.experimental.pallas import tpu as pltpu
from jax.sharding import PartitionSpec as P

MESH = pl.DeviceIdType.MESH
F32 = jnp.float32
BLOCK = 256


def split(x):
    high = x.astype(jnp.bfloat16)
    return high, (x - high.astype(F32)).astype(jnp.bfloat16)


def dot3(a, b):
    (ah, al), (bh, bl) = a, b
    out = jnp.dot(ah, bh, preferred_element_type=F32)
    out += jnp.dot(ah, bl, preferred_element_type=F32)
    return out + jnp.dot(al, bh, preferred_element_type=F32)


def kernel(
    n, m,
    g_hbm, r1_hbm, c1_hbm, r2_hbm, c2_hbm, i1_hbm, i2_hbm,
    panel2_hbm, pivot2_hbm, panel1_hbm, pivot1_hbm,
    g, rows, cols, inv, part, slot, pivot, left, gathered, panel,
    load_sem, ring_send, ring_recv, col_send, col_recv, out_sem, panel_sem,
):
    height, width = g.shape
    nb = inv.shape[-1]
    blocks = width // BLOCK
    chunk = width // n
    half = chunk // 2
    piece = height // m

    row = lax.axis_index("row")
    col = lax.axis_index("col")
    pos = row // 2 + (row % 2) * (n - 1 - 2 * (row // 2))

    def at_position(p):
        p = p % n
        back = p // (n // 2)
        return (1 - back) * 2 * p + back * (2 * n - 2 * p - 1)

    following, preceding = at_position(pos + 1), at_position(pos + n - 1)

    sources = (g_hbm, r2_hbm, c2_hbm, i2_hbm, r1_hbm, c1_hbm, i1_hbm)
    targets = (g, rows.at[0], cols.at[0], inv.at[0], rows.at[1], cols.at[1], inv.at[1])
    loads = [
        pltpu.make_async_copy(s, t, load_sem.at[k]) for k, (s, t) in enumerate(zip(sources, targets))
    ]
    for load in loads:
        load.start()

    barrier = pltpu.get_barrier_semaphore()
    for peer in (following, preceding):
        pl.semaphore_signal(barrier, inc=1, device_id={"row": peer}, device_id_type=MESH)
    for k in range(1, m):
        pl.semaphore_signal(barrier, inc=1, device_id={"col": (col + k) % m}, device_id_type=MESH)
    pl.semaphore_wait(barrier, m + 1)

    pending = []

    def rows_of(index, way):
        return pl.ds(pl.multiple_of((index % n) * chunk + way * half, 8), half)

    def ring_copy(kind, way, step):
        flow = 2 * kind + way
        sign = 1 - 2 * way
        if step < n - 1:
            if step == 0:
                source = part.at[kind, rows_of(pos, way)]
            else:
                source = slot.at[flow, step - 1]
            target = slot.at[flow, step]
        else:
            where = rows_of(pos + n + sign * (1 - (step - n + 1)) + n, way)
            source = pivot.at[kind, where]
            target = pivot.at[kind, where]
        return pltpu.make_async_remote_copy(
            src_ref=source,
            dst_ref=target,
            send_sem=ring_send.at[flow, step],
            recv_sem=ring_recv.at[flow, step],
            device_id={"row": following if way == 0 else preceding},
            device_id_type=MESH,
        )

    outs = (pivot2_hbm, pivot1_hbm)

    def put(kind, way, index):
        flow = 2 * kind + way
        where = rows_of(index, way)
        copy = pltpu.make_async_copy(pivot.at[kind, where], outs[kind].at[where], out_sem.at[flow])
        copy.start()

    def ring_send_step(kind, step):
        for way in range(2):
            copy = ring_copy(kind, way, step)
            copy.start()
            pending.append(copy)

    def ring_step(kind, step):
        for way in range(2):
            flow = 2 * kind + way
            sign = 1 - 2 * way
            ring_copy(kind, way, step).wait_recv()
            if step < n - 1:
                index = pos + 2 * n - sign * (step + 1)
                where = rows_of(index, way)
                total = slot[flow, step] + part[kind, where, :]
                if step < n - 2:
                    slot[flow, step] = total
                else:
                    pivot[kind, where, :] = -dot3(split(total), split(inv[kind]))
            else:
                index = pos + 2 * n - sign * (step - n + 1)
            if step < 2 * n - 3:
                copy = ring_copy(kind, way, step + 1)
                copy.start()
                pending.append(copy)
            if step >= n - 2:
                put(kind, way, index)

    def products(kind):
        @pl.loop(0, blocks)
        def _(k):
            where = pl.ds(pl.multiple_of(k * BLOCK, BLOCK), BLOCK)
            part[kind, where, :] = dot3(split(g[:, where].T), split(rows[kind]))

    def lefts(kind):
        left[...] = jnp.zeros_like(left)

        @pl.loop(0, blocks)
        def _(k):
            where = pl.ds(pl.multiple_of(k * BLOCK, BLOCK), BLOCK)
            left[...] += dot3(split(g[:, where]), split(cols[kind, where, :]))

    def piece_of(index):
        return pl.ds(pl.multiple_of(index * piece, 8), piece)

    def scatter_copy(kind, k):
        return pltpu.make_async_remote_copy(
            src_ref=left.at[piece_of((col + k) % m)],
            dst_ref=gathered.at[kind, k - 1],
            send_sem=col_send.at[kind, 0, k - 1],
            recv_sem=col_recv.at[kind, 0, k - 1],
            device_id={"col": (col + k) % m},
            device_id_type=MESH,
        )

    def gather_copy(kind, k):
        mine = piece_of(col)
        return pltpu.make_async_remote_copy(
            src_ref=panel.at[kind, mine],
            dst_ref=panel.at[kind, mine],
            send_sem=col_send.at[kind, 1, k - 1],
            recv_sem=col_recv.at[kind, 1, k - 1],
            device_id={"col": (col + k) % m},
            device_id_type=MESH,
        )

    def col_scatter(kind):
        for k in range(1, m):
            scatter_copy(kind, k).start()

    def col_gather(kind):
        total = left[piece_of(col), :]
        for k in range(1, m):
            scatter_copy(kind, k).wait_recv()
            total += gathered[kind, k - 1]
        panel[kind, piece_of(col), :] = -dot3(split(total), split(inv[kind]))
        for k in range(1, m):
            gather_copy(kind, k).start()
        for k in range(1, m):
            scatter_copy(kind, k).wait_send()

    panels = (panel2_hbm, panel1_hbm)

    def put_panel(kind):
        return pltpu.make_async_copy(panel.at[kind], panels[kind], panel_sem.at[kind])

    def col_finish(kind):
        for k in range(1, m):
            gather_copy(kind, k).wait_recv()
        put_panel(kind).start()

    loads[0].wait()
    loads[1].wait()
    products(0)
    ring_send_step(0, 0)
    loads[2].wait()
    lefts(0)
    col_scatter(0)
    ring_step(0, 0)
    loads[3].wait()
    col_gather(0)
    ring_step(0, 1)
    col_finish(0)

    @pl.when(col == m - 1)
    def _():
        g[:, width - nb :] += panel[0]

    loads[4].wait()
    products(1)
    ring_send_step(1, 0)
    loads[5].wait()
    lefts(1)
    loads[6].wait()
    col_scatter(1)
    steps = 2 * n - 2
    for step in range(2, steps + 2):
        if step < steps:
            ring_step(0, step)
        ring_step(1, step - 2)
        if step == 4:
            col_gather(1)
        if step == 7:
            col_finish(1)

    for copy in pending:
        copy.wait_send()
    for kind in range(2):
        for k in range(1, m):
            gather_copy(kind, k).wait_send()
        put_panel(kind).wait()
        for way in range(2):
            for _ in range(n):
                where = pl.ds(way * half, half)
                pltpu.make_async_copy(
                    pivot.at[kind, where], outs[kind].at[where], out_sem.at[2 * kind + way]
                ).wait()


def solution(mesh):
    n, m = mesh.shape["row"], mesh.shape["col"]

    def local(g, r1, c1, r2, c2, i1, i2):
        height, width = g.shape
        nb = i1.shape[0]
        half = width // n // 2
        any_space = pl.BlockSpec(memory_space=pl.ANY)
        tall = jax.ShapeDtypeStruct((height, nb), F32)
        wide = jax.ShapeDtypeStruct((width, nb), F32)
        steps = 2 * n - 2
        return pl.pallas_call(
            functools.partial(kernel, n, m),
            out_shape=(tall, wide, tall, wide),
            in_specs=[any_space] * 7,
            out_specs=(any_space,) * 4,
            scratch_shapes=[
                pltpu.VMEM((height, width), F32),
                pltpu.VMEM((2, height, nb), F32),
                pltpu.VMEM((2, width, nb), F32),
                pltpu.VMEM((2, nb, nb), F32),
                pltpu.VMEM((2, width, nb), F32),
                pltpu.VMEM((4, n - 1, half, nb), F32),
                pltpu.VMEM((2, width, nb), F32),
                pltpu.VMEM((height, nb), F32),
                pltpu.VMEM((2, m - 1, height // m, nb), F32),
                pltpu.VMEM((2, height, nb), F32),
                pltpu.SemaphoreType.DMA((7,)),
                pltpu.SemaphoreType.DMA((4, steps)),
                pltpu.SemaphoreType.DMA((4, steps)),
                pltpu.SemaphoreType.DMA((2, 2, m - 1)),
                pltpu.SemaphoreType.DMA((2, 2, m - 1)),
                pltpu.SemaphoreType.DMA((4,)),
                pltpu.SemaphoreType.DMA((2,)),
            ],
            compiler_params=pltpu.CompilerParams(collective_id=0, has_side_effects=True),
        )(g, r1, c1, r2, c2, i1, i2)

    return jax.shard_map(
        local,
        mesh=mesh,
        in_specs=(P("row", "col"), P("row", None), P("col", None), P("row", None), P("col", None), P(), P()),
        out_specs=(P("row", None), P("col", None), P("row", None), P("col", None)),
        check_vma=False,
    )
```

```python
import functools

import jax
import jax.numpy as jnp
from jax import lax
from jax.experimental import pallas as pl
from jax.experimental.pallas import tpu as pltpu
from jax.sharding import PartitionSpec as P

MESH = pl.DeviceIdType.MESH
F32 = jnp.float32
BLOCK = 256
LATE = 5
VMEM_LIMIT = 48 << 20


def split(x):
    high = x.astype(jnp.bfloat16)
    return high, (x - high.astype(F32)).astype(jnp.bfloat16)


def dot3(a, b):
    (ah, al), (bh, bl) = a, b
    out = jnp.dot(ah, bh, preferred_element_type=F32)
    out += jnp.dot(ah, bl, preferred_element_type=F32)
    return out + jnp.dot(al, bh, preferred_element_type=F32)


def kernel(
    n, m,
    g_hbm, r1_hbm, c1_hbm, r2_hbm, c2_hbm, i1_hbm, i2_hbm,
    panel2, pivot2, panel1, pivot1,
    g, rows, cols, inv, part, slot2, slot1, slot_late, left, gathered,
    load_sem, ring_send, ring_recv, col_send, col_recv,
):
    height, width = g.shape
    nb = inv.shape[-1]
    blocks = width // BLOCK
    piece = height // m
    early = width - nb

    row = lax.axis_index("row")
    col = lax.axis_index("col")
    pos = row // 2 + (row % 2) * (n - 1 - 2 * (row // 2))

    def at_position(p):
        p = p % n
        back = p // (n // 2)
        return (1 - back) * 2 * p + back * (2 * n - 2 * p - 1)

    following, preceding = at_position(pos + 1), at_position(pos + n - 1)

    sources = (g_hbm, r2_hbm, r1_hbm, c2_hbm, i2_hbm, c1_hbm, i1_hbm)
    targets = (g, rows.at[0], rows.at[1], cols.at[0], inv.at[0], cols.at[1], inv.at[1])
    loads = [
        pltpu.make_async_copy(s, t, load_sem.at[k]) for k, (s, t) in enumerate(zip(sources, targets))
    ]
    for load in loads:
        load.start()

    barrier = pltpu.get_barrier_semaphore()
    for peer in (following, preceding):
        pl.semaphore_signal(barrier, inc=1, device_id={"row": peer}, device_id_type=MESH)
    for k in range(1, m):
        pl.semaphore_signal(barrier, inc=1, device_id={"col": (col + k) % m}, device_id_type=MESH)

    pending = []

    groups = ((0, 0, width, slot2), (1, 0, early, slot1), (1, early, nb, slot_late))
    pivots = (pivot2, pivot1)
    panels = (panel2, panel1)

    def rows_of(group, index, way):
        _, base, span, _ = groups[group]
        chunk = span // n
        half = chunk // 2
        return pl.ds(pl.multiple_of(base + (index % n) * chunk + way * half, 8), half)

    def ring_copy(group, way, step):
        kind, _, _, slot = groups[group]
        sign = 1 - 2 * way
        if step < n - 1:
            if step == 0:
                source = part.at[kind, rows_of(group, pos, way)]
            else:
                source = slot.at[way, step - 1]
            target = slot.at[way, step]
        else:
            where = rows_of(group, pos + 2 * n + sign * (1 - (step - n + 1)), way)
            source = pivots[kind].at[where]
            target = pivots[kind].at[where]
        return pltpu.make_async_remote_copy(
            src_ref=source,
            dst_ref=target,
            send_sem=ring_send.at[group, way, step],
            recv_sem=ring_recv.at[group, way, step],
            device_id={"row": following if way == 0 else preceding},
            device_id_type=MESH,
        )

    def ring_start(group):
        for way in range(2):
            copy = ring_copy(group, way, 0)
            copy.start()
            pending.append(copy)

    def ring_step(group, step):
        kind, _, _, slot = groups[group]
        for way in range(2):
            sign = 1 - 2 * way
            ring_copy(group, way, step).wait_recv()
            if step < n - 1:
                where = rows_of(group, pos + 2 * n - sign * (step + 1), way)
                total = slot[way, step] + part[kind, where, :]
                if step < n - 2:
                    slot[way, step] = total
                else:
                    pivots[kind][where, :] = -dot3(split(total), split(inv[kind]))
            if step < 2 * n - 3:
                copy = ring_copy(group, way, step + 1)
                copy.start()
                pending.append(copy)

    def block_of(k):
        return pl.ds(pl.multiple_of(k * BLOCK, BLOCK), BLOCK)

    def products(kind, first, last):
        @pl.loop(first, last)
        def _(k):
            part[kind, block_of(k), :] = dot3(split(g[:, block_of(k)].T), split(rows[kind]))

    def lefts(kind, first, last):
        @pl.loop(first, last)
        def _(k):
            left[kind] += dot3(split(g[:, block_of(k)]), split(cols[kind, block_of(k), :]))

    def piece_of(index):
        return pl.ds(pl.multiple_of(index * piece, 8), piece)

    def scatter_copy(kind, k):
        return pltpu.make_async_remote_copy(
            src_ref=left.at[kind, piece_of((col + k) % m)],
            dst_ref=gathered.at[kind, k - 1],
            send_sem=col_send.at[kind, 0, k - 1],
            recv_sem=col_recv.at[kind, 0, k - 1],
            device_id={"col": (col + k) % m},
            device_id_type=MESH,
        )

    def gather_copy(kind, k):
        mine = piece_of(col)
        return pltpu.make_async_remote_copy(
            src_ref=panels[kind].at[mine],
            dst_ref=panels[kind].at[mine],
            send_sem=col_send.at[kind, 1, k - 1],
            recv_sem=col_recv.at[kind, 1, k - 1],
            device_id={"col": (col + k) % m},
            device_id_type=MESH,
        )

    def col_scatter(kind):
        for k in range(1, m):
            scatter_copy(kind, k).start()

    def col_gather(kind):
        total = left[kind, piece_of(col), :]
        for k in range(1, m):
            scatter_copy(kind, k).wait_recv()
            total += gathered[kind, k - 1]
        panels[kind][piece_of(col), :] = -dot3(split(total), split(inv[kind]))
        for k in range(1, m):
            gather_copy(kind, k).start()

    def col_finish(kind):
        for k in range(1, m):
            gather_copy(kind, k).wait_recv()

    left[...] = jnp.zeros_like(left)
    last_block = early // BLOCK
    loads[0].wait()
    loads[1].wait()
    products(0, 0, blocks)
    pl.semaphore_wait(barrier, m + 1)
    ring_start(0)
    loads[2].wait()
    products(1, 0, last_block)
    ring_start(1)
    loads[3].wait()
    lefts(0, 0, blocks)
    col_scatter(0)
    for load in loads[4:]:
        load.wait()
    steps = 2 * n - 2
    late = 0
    for step in range(steps):
        if step >= LATE:
            for _ in range(2):
                if late < steps:
                    ring_step(2, late)
                    late += 1
                if _ == 0:
                    ring_step(0, step)
                else:
                    ring_step(1, step)
        else:
            ring_step(0, step)
            ring_step(1, step)
        if step < 3:
            lefts(1, step * last_block // 3, (step + 1) * last_block // 3)
        if step == 2:
            col_gather(0)
        if step == LATE - 1:
            col_finish(0)

            @pl.when(col == m - 1)
            def _():
                g[:, early:] += panel2[...]

            products(1, last_block, blocks)
            ring_start(2)
            lefts(1, last_block, blocks)
            col_scatter(1)
        if step == LATE + 2:
            col_gather(1)
    while late < steps:
        ring_step(2, late)
        late += 1
    col_finish(1)

    for copy in pending:
        copy.wait_send()
    for kind in range(2):
        for k in range(1, m):
            scatter_copy(kind, k).wait_send()
            gather_copy(kind, k).wait_send()


def write_out(*refs):
    sems = refs[-1]
    copies = [pltpu.make_async_copy(refs[k], refs[4 + k], sems.at[k]) for k in range(4)]
    for copy in copies:
        copy.start()
    for copy in copies:
        copy.wait()


def solution(mesh):
    n, m = mesh.shape["row"], mesh.shape["col"]

    def local(g, r1, c1, r2, c2, i1, i2):
        height, width = g.shape
        nb = i1.shape[0]
        any_space = pl.BlockSpec(memory_space=pl.ANY)
        vmem = pl.BlockSpec(memory_space=pltpu.VMEM)
        shapes = ((height, nb), (width, nb), (height, nb), (width, nb))
        steps = 2 * n - 2
        results = pl.pallas_call(
            functools.partial(kernel, n, m),
            out_shape=tuple(pltpu.VMEM(s, F32) for s in shapes),
            in_specs=[pl.BlockSpec(memory_space=pltpu.HBM)] * 7,
            out_specs=(vmem,) * 4,
            scratch_shapes=[
                pltpu.VMEM((height, width), F32),
                pltpu.VMEM((2, height, nb), F32),
                pltpu.VMEM((2, width, nb), F32),
                pltpu.VMEM((2, nb, nb), F32),
                pltpu.VMEM((2, width, nb), F32),
                pltpu.VMEM((2, n - 1, width // n // 2, nb), F32),
                pltpu.VMEM((2, n - 1, (width - nb) // n // 2, nb), F32),
                pltpu.VMEM((2, n - 1, nb // n // 2, nb), F32),
                pltpu.VMEM((2, height, nb), F32),
                pltpu.VMEM((2, m - 1, height // m, nb), F32),
                pltpu.SemaphoreType.DMA((7,)),
                pltpu.SemaphoreType.DMA((3, 2, steps)),
                pltpu.SemaphoreType.DMA((3, 2, steps)),
                pltpu.SemaphoreType.DMA((2, 2, m - 1)),
                pltpu.SemaphoreType.DMA((2, 2, m - 1)),
            ],
            compiler_params=pltpu.CompilerParams(
                collective_id=0, has_side_effects=True, vmem_limit_bytes=VMEM_LIMIT
            ),
        )(g, r1, c1, r2, c2, i1, i2)
        return pl.pallas_call(
            write_out,
            out_shape=tuple(jax.ShapeDtypeStruct(s, F32) for s in shapes),
            in_specs=[vmem] * 4,
            out_specs=(any_space,) * 4,
            scratch_shapes=[pltpu.SemaphoreType.DMA((4,))],
            compiler_params=pltpu.CompilerParams(vmem_limit_bytes=8 << 20),
        )(*results)

    return jax.shard_map(
        local,
        mesh=mesh,
        in_specs=(P("row", "col"), P("row", None), P("col", None), P("row", None), P("col", None), P(), P()),
        out_specs=(P("row", None), P("col", None), P("row", None), P("col", None)),
        check_vma=False,
    )
```

```python
import functools

import jax
import jax.numpy as jnp
from jax import lax
from jax.experimental import pallas as pl
from jax.experimental.pallas import tpu as pltpu
from jax.sharding import PartitionSpec as P

MESH = pl.DeviceIdType.MESH
F32 = jnp.float32
BLOCK = 256
LATE = 5
VMEM_LIMIT = 48 << 20


def split(x):
    high = x.astype(jnp.bfloat16)
    return high, (x - high.astype(F32)).astype(jnp.bfloat16)


def dot3(a, b):
    (ah, al), (bh, bl) = a, b
    out = jnp.dot(ah, bh, preferred_element_type=F32)
    out += jnp.dot(ah, bl, preferred_element_type=F32)
    return out + jnp.dot(al, bh, preferred_element_type=F32)


def kernel(
    n, m,
    g_hbm, r1_hbm, c1_hbm, r2_hbm, c2_hbm, i1_hbm, i2_hbm,
    panel2, pivot2, panel1, pivot1,
    g, rows, cols, inv, part, slot2, slot1, slot_late, left, gathered,
    load_sem, ring_send, ring_recv, col_send, col_recv,
):
    height, width = g.shape
    nb = inv.shape[-1]
    blocks = width // BLOCK
    piece = height // m
    early = width - nb

    row = lax.axis_index("row")
    col = lax.axis_index("col")
    pos = row // 2 + (row % 2) * (n - 1 - 2 * (row // 2))

    def at_position(p):
        p = p % n
        back = p // (n // 2)
        return (1 - back) * 2 * p + back * (2 * n - 2 * p - 1)

    following, preceding = at_position(pos + 1), at_position(pos + n - 1)

    sources = (g_hbm, r2_hbm, r1_hbm, c2_hbm, i2_hbm, c1_hbm, i1_hbm)
    targets = (g, rows.at[0], rows.at[1], cols.at[0], inv.at[0], cols.at[1], inv.at[1])
    loads = [
        pltpu.make_async_copy(s, t, load_sem.at[k]) for k, (s, t) in enumerate(zip(sources, targets))
    ]
    for load in loads:
        load.start()

    barrier = pltpu.get_barrier_semaphore()
    for peer in (following, preceding):
        pl.semaphore_signal(barrier, inc=1, device_id={"row": peer}, device_id_type=MESH)
    for k in range(1, m):
        pl.semaphore_signal(barrier, inc=1, device_id={"col": (col + k) % m}, device_id_type=MESH)

    pending = []

    parts = slot2.shape[0]
    groups = []
    for q in range(parts):
        groups += [(0, 0, width, parts, q, slot2.at[q]), (1, 0, early, parts, q, slot1.at[q])]
    groups.append((1, early, nb, 1, 0, slot_late))
    late_group = 2 * parts
    pivots = (pivot2, pivot1)
    panels = (panel2, panel1)

    def rows_of(group, index, way):
        _, base, span, cut, q, _ = groups[group]
        chunk = span // n
        size = chunk // 2 // cut
        return pl.ds(pl.multiple_of(base + (index % n) * chunk + (way * cut + q) * size, 8), size)

    def ring_copy(group, way, step):
        kind, _, _, _, _, slot = groups[group]
        sign = 1 - 2 * way
        if step < n - 1:
            if step == 0:
                source = part.at[kind, rows_of(group, pos, way)]
            else:
                source = slot.at[way, step - 1]
            target = slot.at[way, step]
        else:
            where = rows_of(group, pos + 2 * n + sign * (1 - (step - n + 1)), way)
            source = pivots[kind].at[where]
            target = pivots[kind].at[where]
        return pltpu.make_async_remote_copy(
            src_ref=source,
            dst_ref=target,
            send_sem=ring_send.at[group, way, step],
            recv_sem=ring_recv.at[group, way, step],
            device_id={"row": following if way == 0 else preceding},
            device_id_type=MESH,
        )

    def ring_start(group):
        for way in range(2):
            copy = ring_copy(group, way, 0)
            copy.start()
            pending.append(copy)

    def ring_step(group, step):
        kind, _, _, _, _, slot = groups[group]
        for way in range(2):
            sign = 1 - 2 * way
            ring_copy(group, way, step).wait_recv()
            if step < n - 1:
                where = rows_of(group, pos + 2 * n - sign * (step + 1), way)
                total = slot[way, step] + part[kind, where, :]
                if step < n - 2:
                    slot[way, step] = total
                else:
                    pivots[kind][where, :] = -dot3(split(total), split(inv[kind]))
            if step < 2 * n - 3:
                copy = ring_copy(group, way, step + 1)
                copy.start()
                pending.append(copy)

    def block_of(k):
        return pl.ds(pl.multiple_of(k * BLOCK, BLOCK), BLOCK)

    def products(kind, first, last, start=0, count=blocks):
        @pl.loop(first, last)
        def _(k):
            where = block_of((start + k) % count)
            part[kind, where, :] = dot3(split(g[:, where].T), split(rows[kind]))

    def lefts(kind, first, last):
        @pl.loop(first, last)
        def _(k):
            left[kind] += dot3(split(g[:, block_of(k)]), split(cols[kind, block_of(k), :]))

    def piece_of(index):
        return pl.ds(pl.multiple_of(index * piece, 8), piece)

    def scatter_copy(kind, k):
        return pltpu.make_async_remote_copy(
            src_ref=left.at[kind, piece_of((col + k) % m)],
            dst_ref=gathered.at[kind, k - 1],
            send_sem=col_send.at[kind, 0, k - 1],
            recv_sem=col_recv.at[kind, 0, k - 1],
            device_id={"col": (col + k) % m},
            device_id_type=MESH,
        )

    def gather_copy(kind, k):
        mine = piece_of(col)
        return pltpu.make_async_remote_copy(
            src_ref=panels[kind].at[mine],
            dst_ref=panels[kind].at[mine],
            send_sem=col_send.at[kind, 1, k - 1],
            recv_sem=col_recv.at[kind, 1, k - 1],
            device_id={"col": (col + k) % m},
            device_id_type=MESH,
        )

    def col_scatter(kind):
        for k in range(1, m):
            scatter_copy(kind, k).start()

    def col_gather(kind):
        total = left[kind, piece_of(col), :]
        for k in range(1, m):
            scatter_copy(kind, k).wait_recv()
            total += gathered[kind, k - 1]
        panels[kind][piece_of(col), :] = -dot3(split(total), split(inv[kind]))
        for k in range(1, m):
            gather_copy(kind, k).start()

    def col_finish(kind):
        for k in range(1, m):
            gather_copy(kind, k).wait_recv()

    left[...] = jnp.zeros_like(left)
    last_block = early // BLOCK
    loads[0].wait()
    loads[1].wait()
    first0 = pos * (width // n) // BLOCK
    first1 = pos * (early // n) // BLOCK
    products(0, 0, 2, first0)
    pl.semaphore_wait(barrier, m + 1)
    for q in range(parts):
        ring_start(2 * q)
    loads[2].wait()
    products(1, 0, 2, first1, last_block)
    for q in range(parts):
        ring_start(2 * q + 1)
    products(0, 2, blocks, first0)
    products(1, 2, last_block, first1, last_block)
    loads[3].wait()
    lefts(0, 0, blocks)
    col_scatter(0)
    for load in loads[4:]:
        load.wait()
    steps = 2 * n - 2
    late = 0
    for step in range(steps):
        for kind in range(2):
            if step >= LATE and late < steps:
                ring_step(late_group, late)
                late += 1
            for q in range(parts):
                ring_step(2 * q + kind, step)
        if step < 3:
            lefts(1, step * last_block // 3, (step + 1) * last_block // 3)
        if step == 2:
            col_gather(0)
        if step == LATE - 1:
            col_finish(0)

            @pl.when(col == m - 1)
            def _():
                g[:, early:] += panel2[...]

            products(1, last_block, blocks)
            ring_start(late_group)
            lefts(1, last_block, blocks)
            col_scatter(1)
        if step == LATE + 2:
            col_gather(1)
    while late < steps:
        ring_step(late_group, late)
        late += 1
    col_finish(1)

    for copy in pending:
        copy.wait_send()
    for kind in range(2):
        for k in range(1, m):
            scatter_copy(kind, k).wait_send()
            gather_copy(kind, k).wait_send()


def write_out(*refs):
    sems = refs[-1]
    copies = [pltpu.make_async_copy(refs[k], refs[4 + k], sems.at[k]) for k in range(4)]
    for copy in copies:
        copy.start()
    for copy in copies:
        copy.wait()


def solution(mesh):
    n, m = mesh.shape["row"], mesh.shape["col"]

    def local(g, r1, c1, r2, c2, i1, i2):
        height, width = g.shape
        nb = i1.shape[0]
        any_space = pl.BlockSpec(memory_space=pl.ANY)
        vmem = pl.BlockSpec(memory_space=pltpu.VMEM)
        shapes = ((height, nb), (width, nb), (height, nb), (width, nb))
        steps = 2 * n - 2
        parts = 1 if any(w % (32 * n) for w in (width, width - nb)) else 2
        results = pl.pallas_call(
            functools.partial(kernel, n, m),
            out_shape=tuple(pltpu.VMEM(s, F32) for s in shapes),
            in_specs=[pl.BlockSpec(memory_space=pltpu.HBM)] * 7,
            out_specs=(vmem,) * 4,
            scratch_shapes=[
                pltpu.VMEM((height, width), F32),
                pltpu.VMEM((2, height, nb), F32),
                pltpu.VMEM((2, width, nb), F32),
                pltpu.VMEM((2, nb, nb), F32),
                pltpu.VMEM((2, width, nb), F32),
                pltpu.VMEM((parts, 2, n - 1, width // n // 2 // parts, nb), F32),
                pltpu.VMEM((parts, 2, n - 1, (width - nb) // n // 2 // parts, nb), F32),
                pltpu.VMEM((2, n - 1, nb // n // 2, nb), F32),
                pltpu.VMEM((2, height, nb), F32),
                pltpu.VMEM((2, m - 1, height // m, nb), F32),
                pltpu.SemaphoreType.DMA((7,)),
                pltpu.SemaphoreType.DMA((2 * parts + 1, 2, steps)),
                pltpu.SemaphoreType.DMA((2 * parts + 1, 2, steps)),
                pltpu.SemaphoreType.DMA((2, 2, m - 1)),
                pltpu.SemaphoreType.DMA((2, 2, m - 1)),
            ],
            compiler_params=pltpu.CompilerParams(
                collective_id=0, has_side_effects=True, vmem_limit_bytes=VMEM_LIMIT
            ),
        )(*[pltpu.with_memory_space_constraint(x, pltpu.HBM) for x in (g, r1, c1, r2, c2, i1, i2)])
        return pl.pallas_call(
            write_out,
            out_shape=tuple(jax.ShapeDtypeStruct(s, F32) for s in shapes),
            in_specs=[vmem] * 4,
            out_specs=(any_space,) * 4,
            scratch_shapes=[pltpu.SemaphoreType.DMA((4,))],
            compiler_params=pltpu.CompilerParams(vmem_limit_bytes=8 << 20),
        )(*results)

    return jax.shard_map(
        local,
        mesh=mesh,
        in_specs=(P("row", "col"), P("row", None), P("col", None), P("row", None), P("col", None), P(), P()),
        out_specs=(P("row", None), P("col", None), P("row", None), P("col", None)),
        check_vma=False,
    )
```

```python
import functools

import jax
import jax.numpy as jnp
from jax import lax
from jax.experimental import pallas as pl
from jax.experimental.pallas import tpu as pltpu
from jax.sharding import PartitionSpec as P

MESH = pl.DeviceIdType.MESH
F32 = jnp.float32
BLOCK = 256
LATE = 5
PIECES = 4
VMEM_LIMIT = 48 << 20


def split(x):
    high = x.astype(jnp.bfloat16)
    return high, (x - high.astype(F32)).astype(jnp.bfloat16)


def dot3(a, b):
    (ah, al), (bh, bl) = a, b
    out = jnp.dot(ah, bh, preferred_element_type=F32)
    out += jnp.dot(ah, bl, preferred_element_type=F32)
    return out + jnp.dot(al, bh, preferred_element_type=F32)


def kernel(
    n, m,
    g_hbm, r1_hbm, c1_hbm, r2_hbm, c2_hbm, i1_hbm, i2_hbm,
    panel2, pivot2, panel1, pivot1,
    g, rows, cols, inv, part, slot2, slot1, slot_late, left, gathered,
    tile_sem, load_sem, ring_send, ring_recv, col_send, col_recv,
):
    height, width = g.shape
    nb = inv.shape[-1]
    blocks = width // BLOCK
    piece = height // m
    early = width - nb

    row = lax.axis_index("row")
    col = lax.axis_index("col")
    pos = row // 2 + (row % 2) * (n - 1 - 2 * (row // 2))

    def at_position(p):
        p = p % n
        back = p // (n // 2)
        return (1 - back) * 2 * p + back * (2 * n - 2 * p - 1)

    following, preceding = at_position(pos + 1), at_position(pos + n - 1)

    first0 = pos * (width // n) // BLOCK
    first1 = pos * (early // n) // BLOCK

    def block_of(k):
        return pl.ds(pl.multiple_of(k * BLOCK, BLOCK), BLOCK)

    def tile_load(k):
        where = block_of((first0 + k) % blocks)
        return pltpu.make_async_copy(g_hbm.at[:, where], g.at[:, where], tile_sem.at[k])

    sources = (r2_hbm, r1_hbm, c2_hbm, i2_hbm, c1_hbm, i1_hbm)
    targets = (rows.at[0], rows.at[1], cols.at[0], inv.at[0], cols.at[1], inv.at[1])
    loads = [
        pltpu.make_async_copy(s, t, load_sem.at[k]) for k, (s, t) in enumerate(zip(sources, targets))
    ]
    loads[0].start()
    for k in range(blocks):
        tile_load(k).start()
    for load in loads[1:]:
        load.start()

    barrier = pltpu.get_barrier_semaphore()
    for peer in (following, preceding):
        pl.semaphore_signal(barrier, inc=1, device_id={"row": peer}, device_id_type=MESH)
    for k in range(1, m):
        pl.semaphore_signal(barrier, inc=1, device_id={"col": (col + k) % m}, device_id_type=MESH)

    pending = []

    parts = slot2.shape[0]
    groups = []
    for q in range(parts):
        groups += [(0, 0, width, parts, q, slot2.at[q]), (1, 0, early, parts, q, slot1.at[q])]
    groups.append((1, early, nb, 1, 0, slot_late))
    late_group = 2 * parts
    pivots = (pivot2, pivot1)
    panels = (panel2, panel1)

    def rows_of(group, index, way):
        _, base, span, cut, q, _ = groups[group]
        chunk = span // n
        size = chunk // 2 // cut
        return pl.ds(pl.multiple_of(base + (index % n) * chunk + (way * cut + q) * size, 8), size)

    def ring_copy(group, way, step):
        kind, _, _, _, _, slot = groups[group]
        sign = 1 - 2 * way
        if step < n - 1:
            if step == 0:
                source = part.at[kind, rows_of(group, pos, way)]
            else:
                source = slot.at[way, step - 1]
            target = slot.at[way, step]
        else:
            where = rows_of(group, pos + 2 * n + sign * (1 - (step - n + 1)), way)
            source = pivots[kind].at[where]
            target = pivots[kind].at[where]
        return pltpu.make_async_remote_copy(
            src_ref=source,
            dst_ref=target,
            send_sem=ring_send.at[group, way, step],
            recv_sem=ring_recv.at[group, way, step],
            device_id={"row": following if way == 0 else preceding},
            device_id_type=MESH,
        )

    def ring_start(group):
        for way in range(2):
            copy = ring_copy(group, way, 0)
            copy.start()
            pending.append(copy)

    def ring_step(group, step):
        kind, _, _, _, _, slot = groups[group]
        for way in range(2):
            sign = 1 - 2 * way
            ring_copy(group, way, step).wait_recv()
            if step < n - 1:
                where = rows_of(group, pos + 2 * n - sign * (step + 1), way)
                total = slot[way, step] + part[kind, where, :]
                if step < n - 2:
                    slot[way, step] = total
                else:
                    pivots[kind][where, :] = -dot3(split(total), split(inv[kind]))
            if step < 2 * n - 3:
                copy = ring_copy(group, way, step + 1)
                copy.start()
                pending.append(copy)

    def products(kind, first, last, start=0, count=blocks):
        @pl.loop(first, last)
        def _(k):
            where = block_of((start + k) % count)
            part[kind, where, :] = dot3(split(g[:, where].T), split(rows[kind]))

    def lefts(kind, first, last):
        @pl.loop(first, last)
        def _(k):
            left[kind] += dot3(split(g[:, block_of(k)]), split(cols[kind, block_of(k), :]))

    def piece_of(index):
        return pl.ds(pl.multiple_of(index * piece, 8), piece)

    def scatter_copy(kind, k):
        return pltpu.make_async_remote_copy(
            src_ref=left.at[kind, piece_of((col + k) % m)],
            dst_ref=gathered.at[kind, k - 1],
            send_sem=col_send.at[kind, 0, k - 1],
            recv_sem=col_recv.at[kind, 0, k - 1],
            device_id={"col": (col + k) % m},
            device_id_type=MESH,
        )

    def gather_copy(kind, k):
        mine = piece_of(col)
        return pltpu.make_async_remote_copy(
            src_ref=panels[kind].at[mine],
            dst_ref=panels[kind].at[mine],
            send_sem=col_send.at[kind, 1, k - 1],
            recv_sem=col_recv.at[kind, 1, k - 1],
            device_id={"col": (col + k) % m},
            device_id_type=MESH,
        )

    def col_scatter(kind):
        for k in range(1, m):
            scatter_copy(kind, k).start()

    def col_gather(kind):
        total = left[kind, piece_of(col), :]
        for k in range(1, m):
            scatter_copy(kind, k).wait_recv()
            total += gathered[kind, k - 1]
        panels[kind][piece_of(col), :] = -dot3(split(total), split(inv[kind]))
        for k in range(1, m):
            gather_copy(kind, k).start()

    def col_finish(kind):
        for k in range(1, m):
            gather_copy(kind, k).wait_recv()

    left[...] = jnp.zeros_like(left)
    last_block = early // BLOCK
    loads[0].wait()
    tile_load(0).wait()
    tile_load(1).wait()
    products(0, 0, 2, first0)
    pl.semaphore_wait(barrier, m + 1)
    for q in range(parts):
        ring_start(2 * q)
    for k in range(2, blocks):
        tile_load(k).wait()
    loads[1].wait()
    products(1, 0, 2, first1, last_block)
    for q in range(parts):
        ring_start(2 * q + 1)
    products(0, 2, blocks, first0)
    products(1, 2, last_block, first1, last_block)
    for load in loads[2:]:
        load.wait()
    steps = 2 * n - 2
    late = 0
    for step in range(steps):
        for kind in range(2):
            if step >= LATE and late < steps:
                ring_step(late_group, late)
                late += 1
            for q in range(parts):
                ring_step(2 * q + kind, step)
            if step == 0:
                lefts(0, kind * (blocks // 2), blocks if kind else blocks // 2)
        if step == 0:
            col_scatter(0)
        elif step < 4:
            lefts(1, (step - 1) * last_block // 3, step * last_block // 3)
        if step == 2:
            col_gather(0)
        if step == LATE - 1:
            col_finish(0)

            @pl.when(col == m - 1)
            def _():
                g[:, early:] += panel2[...]

            products(1, last_block, blocks)
            ring_start(late_group)
            lefts(1, last_block, blocks)
            col_scatter(1)
        if step == LATE + 2:
            col_gather(1)
    while late < steps:
        ring_step(late_group, late)
        late += 1
    col_finish(1)

    for copy in pending:
        copy.wait_send()
    for kind in range(2):
        for k in range(1, m):
            scatter_copy(kind, k).wait_send()
            gather_copy(kind, k).wait_send()


def write_out(*refs):
    sems = refs[-1]
    copies = []
    for k in range(4):
        size = refs[k].shape[0] // PIECES
        for p in range(PIECES):
            where = pl.ds(p * size, size)
            copies.append(pltpu.make_async_copy(refs[k].at[where], refs[4 + k].at[where], sems.at[k, p]))
    for copy in copies:
        copy.start()
    for copy in copies:
        copy.wait()


def solution(mesh):
    n, m = mesh.shape["row"], mesh.shape["col"]

    def local(g, r1, c1, r2, c2, i1, i2):
        height, width = g.shape
        nb = i1.shape[0]
        any_space = pl.BlockSpec(memory_space=pl.ANY)
        vmem = pl.BlockSpec(memory_space=pltpu.VMEM)
        shapes = ((height, nb), (width, nb), (height, nb), (width, nb))
        steps = 2 * n - 2
        parts = 1 if any(w % (32 * n) for w in (width, width - nb)) else 2
        results = pl.pallas_call(
            functools.partial(kernel, n, m),
            out_shape=tuple(pltpu.VMEM(s, F32) for s in shapes),
            in_specs=[pl.BlockSpec(memory_space=pltpu.HBM)] * 7,
            out_specs=(vmem,) * 4,
            scratch_shapes=[
                pltpu.VMEM((height, width), F32),
                pltpu.VMEM((2, height, nb), F32),
                pltpu.VMEM((2, width, nb), F32),
                pltpu.VMEM((2, nb, nb), F32),
                pltpu.VMEM((2, width, nb), F32),
                pltpu.VMEM((parts, 2, n - 1, width // n // 2 // parts, nb), F32),
                pltpu.VMEM((parts, 2, n - 1, (width - nb) // n // 2 // parts, nb), F32),
                pltpu.VMEM((2, n - 1, nb // n // 2, nb), F32),
                pltpu.VMEM((2, height, nb), F32),
                pltpu.VMEM((2, m - 1, height // m, nb), F32),
                pltpu.SemaphoreType.DMA((width // BLOCK,)),
                pltpu.SemaphoreType.DMA((6,)),
                pltpu.SemaphoreType.DMA((2 * parts + 1, 2, steps)),
                pltpu.SemaphoreType.DMA((2 * parts + 1, 2, steps)),
                pltpu.SemaphoreType.DMA((2, 2, m - 1)),
                pltpu.SemaphoreType.DMA((2, 2, m - 1)),
            ],
            compiler_params=pltpu.CompilerParams(
                collective_id=0, has_side_effects=True, vmem_limit_bytes=VMEM_LIMIT
            ),
        )(*[pltpu.with_memory_space_constraint(x, pltpu.HBM) for x in (g, r1, c1, r2, c2, i1, i2)])
        return pl.pallas_call(
            write_out,
            out_shape=tuple(jax.ShapeDtypeStruct(s, F32) for s in shapes),
            in_specs=[vmem] * 4,
            out_specs=(any_space,) * 4,
            scratch_shapes=[pltpu.SemaphoreType.DMA((4, PIECES))],
            compiler_params=pltpu.CompilerParams(vmem_limit_bytes=8 << 20),
        )(*results)

    return jax.shard_map(
        local,
        mesh=mesh,
        in_specs=(P("row", "col"), P("row", None), P("col", None), P("row", None), P("col", None), P(), P()),
        out_specs=(P("row", None), P("col", None), P("row", None), P("col", None)),
        check_vma=False,
    )
```

```python
import functools

import jax
import jax.numpy as jnp
from jax import lax
from jax.experimental import pallas as pl
from jax.experimental.pallas import tpu as pltpu
from jax.sharding import PartitionSpec as P

MESH = pl.DeviceIdType.MESH
F32 = jnp.float32
BLOCK = 256
LATE = 6
PIECES = 4
VMEM_LIMIT = 48 << 20


def split(x):
    high = x.astype(jnp.bfloat16)
    return high, (x - high.astype(F32)).astype(jnp.bfloat16)


def dot3(a, b):
    (ah, al), (bh, bl) = a, b
    out = jnp.dot(ah, bh, preferred_element_type=F32)
    out += jnp.dot(ah, bl, preferred_element_type=F32)
    return out + jnp.dot(al, bh, preferred_element_type=F32)


def kernel(
    n, m,
    g_hbm, r1_hbm, c1_hbm, r2_hbm, c2_hbm, i1_hbm, i2_hbm,
    panel2, pivot2, panel1, pivot1,
    g, rows, cols, inv, part, slot2, slot1, slot_late, left, gathered,
    tile_sem, load_sem, ring_send, ring_recv, col_send, col_recv,
):
    height, width = g.shape
    nb = inv.shape[-1]
    blocks = width // BLOCK
    piece = height // m
    early = width - nb

    row = lax.axis_index("row")
    col = lax.axis_index("col")
    pos = row // 2 + (row % 2) * (n - 1 - 2 * (row // 2))

    def at_position(p):
        p = p % n
        back = p // (n // 2)
        return (1 - back) * 2 * p + back * (2 * n - 2 * p - 1)

    following, preceding = at_position(pos + 1), at_position(pos + n - 1)

    first0 = pos * (width // n) // BLOCK
    first1 = pos * (early // n) // BLOCK

    def block_of(k):
        return pl.ds(pl.multiple_of(k * BLOCK, BLOCK), BLOCK)

    def tile_load(k):
        where = block_of((first0 + k) % blocks)
        return pltpu.make_async_copy(g_hbm.at[:, where], g.at[:, where], tile_sem.at[k])

    sources = (r2_hbm, r1_hbm, c2_hbm, i2_hbm, c1_hbm, i1_hbm)
    targets = (rows.at[0], rows.at[1], cols.at[0], inv.at[0], cols.at[1], inv.at[1])
    loads = [
        pltpu.make_async_copy(s, t, load_sem.at[k]) for k, (s, t) in enumerate(zip(sources, targets))
    ]
    loads[0].start()
    for k in range(blocks):
        tile_load(k).start()
    for load in loads[1:]:
        load.start()

    barrier = pltpu.get_barrier_semaphore()
    for peer in (following, preceding):
        pl.semaphore_signal(barrier, inc=1, device_id={"row": peer}, device_id_type=MESH)
    for k in range(1, m):
        pl.semaphore_signal(barrier, inc=1, device_id={"col": (col + k) % m}, device_id_type=MESH)

    pending = []

    parts = slot2.shape[0]
    groups = []
    for q in range(parts):
        groups += [(0, 0, width, parts, q, slot2.at[q]), (1, 0, early, parts, q, slot1.at[q])]
    groups.append((1, early, nb, 1, 0, slot_late))
    late_group = 2 * parts
    pivots = (pivot2, pivot1)
    panels = (panel2, panel1)

    def rows_of(group, index, way):
        _, base, span, cut, q, _ = groups[group]
        chunk = span // n
        size = chunk // 2 // cut
        return pl.ds(pl.multiple_of(base + (index % n) * chunk + (way * cut + q) * size, 8), size)

    def ring_copy(group, way, step):
        kind, _, _, _, _, slot = groups[group]
        sign = 1 - 2 * way
        if step < n - 1:
            if step == 0:
                source = part.at[kind, rows_of(group, pos, way)]
            else:
                source = slot.at[way, step - 1]
            target = slot.at[way, step]
        else:
            where = rows_of(group, pos + 2 * n + sign * (1 - (step - n + 1)), way)
            source = pivots[kind].at[where]
            target = pivots[kind].at[where]
        return pltpu.make_async_remote_copy(
            src_ref=source,
            dst_ref=target,
            send_sem=ring_send.at[group, way, step],
            recv_sem=ring_recv.at[group, way, step],
            device_id={"row": following if way == 0 else preceding},
            device_id_type=MESH,
        )

    def ring_start(group):
        for way in range(2):
            copy = ring_copy(group, way, 0)
            copy.start()
            pending.append(copy)

    def ring_step(group, step):
        kind, _, _, _, _, slot = groups[group]
        for way in range(2):
            sign = 1 - 2 * way
            ring_copy(group, way, step).wait_recv()
            if step < n - 1:
                where = rows_of(group, pos + 2 * n - sign * (step + 1), way)
                total = slot[way, step] + part[kind, where, :]
                if step < n - 2:
                    slot[way, step] = total
                else:
                    pivots[kind][where, :] = -dot3(split(total), split(inv[kind]))
            if step < 2 * n - 3:
                copy = ring_copy(group, way, step + 1)
                copy.start()
                pending.append(copy)

    def products(kind, first, last, start=0, count=blocks):
        @pl.loop(first, last)
        def _(k):
            where = block_of((start + k) % count)
            part[kind, where, :] = dot3(split(g[:, where].T), split(rows[kind]))

    def lefts(kind, first, last):
        @pl.loop(first, last)
        def _(k):
            left[kind] += dot3(split(g[:, block_of(k)]), split(cols[kind, block_of(k), :]))

    def piece_of(index):
        return pl.ds(pl.multiple_of(index * piece, 8), piece)

    def scatter_copy(kind, k):
        return pltpu.make_async_remote_copy(
            src_ref=left.at[kind, piece_of((col + k) % m)],
            dst_ref=gathered.at[kind, k - 1],
            send_sem=col_send.at[kind, 0, k - 1],
            recv_sem=col_recv.at[kind, 0, k - 1],
            device_id={"col": (col + k) % m},
            device_id_type=MESH,
        )

    def gather_copy(kind, k):
        mine = piece_of(col)
        return pltpu.make_async_remote_copy(
            src_ref=panels[kind].at[mine],
            dst_ref=panels[kind].at[mine],
            send_sem=col_send.at[kind, 1, k - 1],
            recv_sem=col_recv.at[kind, 1, k - 1],
            device_id={"col": (col + k) % m},
            device_id_type=MESH,
        )

    def col_scatter(kind):
        for k in range(1, m):
            scatter_copy(kind, k).start()

    def col_gather(kind):
        total = left[kind, piece_of(col), :]
        for k in range(1, m):
            scatter_copy(kind, k).wait_recv()
            total += gathered[kind, k - 1]
        panels[kind][piece_of(col), :] = -dot3(split(total), split(inv[kind]))
        for k in range(1, m):
            gather_copy(kind, k).start()

    def col_finish(kind):
        for k in range(1, m):
            gather_copy(kind, k).wait_recv()

    left[...] = jnp.zeros_like(left)
    last_block = early // BLOCK
    loads[0].wait()
    tile_load(0).wait()
    tile_load(1).wait()
    products(0, 0, 2, first0)
    pl.semaphore_wait(barrier, m + 1)
    for q in range(parts):
        ring_start(2 * q)
    for k in range(2, blocks):
        tile_load(k).wait()
    loads[1].wait()
    products(1, 0, 2, first1, last_block)
    for q in range(parts):
        ring_start(2 * q + 1)
    products(0, 2, blocks, first0)
    products(1, 2, last_block, first1, last_block)
    for load in loads[2:]:
        load.wait()
    steps = 2 * n - 2
    late = 0
    for step in range(steps):
        for kind in range(2):
            if step >= LATE and late < steps:
                ring_step(late_group, late)
                late += 1
            for q in range(parts):
                ring_step(2 * q + kind, step)
            if step == 0:
                lefts(0, kind * (blocks // 2), blocks if kind else blocks // 2)
        if step == 0:
            col_scatter(0)
        elif step < 4:
            lefts(1, (step - 1) * last_block // 3, step * last_block // 3)
        if step == 3:
            col_gather(0)
        if step == LATE - 1:
            col_finish(0)

            @pl.when(col == m - 1)
            def _():
                g[:, early:] += panel2[...]

            products(1, last_block, blocks)
            ring_start(late_group)
            lefts(1, last_block, blocks)
            col_scatter(1)
        if step == LATE + 2:
            col_gather(1)
    while late < steps:
        ring_step(late_group, late)
        late += 1
    col_finish(1)

    for copy in pending:
        copy.wait_send()
    for kind in range(2):
        for k in range(1, m):
            scatter_copy(kind, k).wait_send()
            gather_copy(kind, k).wait_send()


def write_out(*refs):
    sems = refs[-1]
    copies = []
    for k in range(4):
        size = refs[k].shape[0] // PIECES
        for p in range(PIECES):
            where = pl.ds(p * size, size)
            copies.append(pltpu.make_async_copy(refs[k].at[where], refs[4 + k].at[where], sems.at[k, p]))
    for copy in copies:
        copy.start()
    for copy in copies:
        copy.wait()


def solution(mesh):
    n, m = mesh.shape["row"], mesh.shape["col"]

    def local(g, r1, c1, r2, c2, i1, i2):
        height, width = g.shape
        nb = i1.shape[0]
        any_space = pl.BlockSpec(memory_space=pl.ANY)
        vmem = pl.BlockSpec(memory_space=pltpu.VMEM)
        shapes = ((height, nb), (width, nb), (height, nb), (width, nb))
        steps = 2 * n - 2
        parts = 1
        results = pl.pallas_call(
            functools.partial(kernel, n, m),
            out_shape=tuple(pltpu.VMEM(s, F32) for s in shapes),
            in_specs=[pl.BlockSpec(memory_space=pltpu.HBM)] * 7,
            out_specs=(vmem,) * 4,
            scratch_shapes=[
                pltpu.VMEM((height, width), F32),
                pltpu.VMEM((2, height, nb), F32),
                pltpu.VMEM((2, width, nb), F32),
                pltpu.VMEM((2, nb, nb), F32),
                pltpu.VMEM((2, width, nb), F32),
                pltpu.VMEM((parts, 2, n - 1, width // n // 2 // parts, nb), F32),
                pltpu.VMEM((parts, 2, n - 1, (width - nb) // n // 2 // parts, nb), F32),
                pltpu.VMEM((2, n - 1, nb // n // 2, nb), F32),
                pltpu.VMEM((2, height, nb), F32),
                pltpu.VMEM((2, m - 1, height // m, nb), F32),
                pltpu.SemaphoreType.DMA((width // BLOCK,)),
                pltpu.SemaphoreType.DMA((6,)),
                pltpu.SemaphoreType.DMA((2 * parts + 1, 2, steps)),
                pltpu.SemaphoreType.DMA((2 * parts + 1, 2, steps)),
                pltpu.SemaphoreType.DMA((2, 2, m - 1)),
                pltpu.SemaphoreType.DMA((2, 2, m - 1)),
            ],
            compiler_params=pltpu.CompilerParams(
                collective_id=0, has_side_effects=True, vmem_limit_bytes=VMEM_LIMIT
            ),
        )(*[pltpu.with_memory_space_constraint(x, pltpu.HBM) for x in (g, r1, c1, r2, c2, i1, i2)])
        return pl.pallas_call(
            write_out,
            out_shape=tuple(jax.ShapeDtypeStruct(s, F32) for s in shapes),
            in_specs=[vmem] * 4,
            out_specs=(any_space,) * 4,
            scratch_shapes=[pltpu.SemaphoreType.DMA((4, PIECES))],
            compiler_params=pltpu.CompilerParams(vmem_limit_bytes=8 << 20),
        )(*results)

    return jax.shard_map(
        local,
        mesh=mesh,
        in_specs=(P("row", "col"), P("row", None), P("col", None), P("row", None), P("col", None), P(), P()),
        out_specs=(P("row", None), P("col", None), P("row", None), P("col", None)),
        check_vma=False,
    )
```
